256 devices in a mesh: tm: 8 (over y, x_lo), space: 32 (over z, x_hi, core).
Axes of the slice: x: 4 (x_hi: 2, x_lo: 2; x = x_hi * 2 + x_lo), y: 4, z: 8, core: 2. Of those that a mesh axis runs over, the one named last changes fastest.
Arguments:
- density: float32 [128, 512, 1024], P('tm', 'space'), may hold values from 0.2 to 2
- flux_x: float32 [128, 512, 1024], P('tm', 'space'), may hold values from -3 to 3
- flux_y: float32 [128, 512, 1024], P('tm', 'space'), may hold values from -3 to 3
- source: float32 [128, 512, 1024], P('tm', 'space'), may hold values from -3 to 3
- potential: float32 [128, 512, 1024], P('tm', 'space'), may hold values from -6 to 6
- start_density: float32 [512, 1024], P('space'), may hold values from 0.2 to 2
- end_density: float32 [512, 1024], P('space'), may hold values from 0.2 to 2
Outputs:
- final_density: float32 [128, 512, 1024], P('tm', 'space')
- final_flux_x: float32 [128, 512, 1024], P('tm', 'space')
- final_flux_y: float32 [128, 512, 1024], P('tm', 'space')
- final_source: float32 [128, 512, 1024], P('tm', 'space')
- final_potential: float32 [128, 512, 1024], P('tm', 'space')
The draws below stay inside these ranges and needn't reach their ends.
All inputs are finite; a program needn't handle non-finite values.
Results may differ from the reference program's by a relative error of at most 0.00002.
Values sent between devices are 32-bit elements; how exact they have to be, the bound alone decides.
A program may use at most 64 MiB of HBM per device.

```python
import jax
import jax.numpy as jnp
from jax import lax

NY = 1024
NEWTON = 8
ITERS = 6
STEPS = 128
NX = 512


def shard_levels(own_key, shape, split, smallest, largest):
    factor_of = 1.0
    for dim, shards_of in split:
        heights = jax.random.uniform(jax.random.fold_in(jax.random.fold_in(own_key, 6), dim), (shards_of,), jnp.float32, smallest / len(split), largest / len(split))
        factor_of = factor_of * jnp.repeat(jnp.exp(heights), shape[dim] // shards_of).reshape((-1,) + (1,) * (len(shape) - 1 - dim))
    return factor_of


def noise(own_key, extent, scale, most, shards=(), dtype=jnp.bfloat16):
    factor_of = shard_levels(own_key, extent, shards, -0.22, 0.18) if shards else 1.0
    array = jax.random.normal(own_key, extent, jnp.float32) * scale * factor_of
    return jnp.minimum(jnp.maximum(array, -most), most).astype(dtype)


def setup_inputs(seed: int = 0) -> dict:
    keys = jax.random.split(jax.random.key(seed), 8)
    return {
        "density": jnp.clip(0.2 + 1.8 * jax.random.uniform(keys[0], (STEPS, NX, NY), jnp.float32) ** shard_levels(keys[0], (STEPS, NX, NY), ((0, 8), (1, 32)), -0.2, 0.2), 0.2, 2.0),
        "flux_x": noise(keys[1], (STEPS, NX, NY), 0.5, 3.0, ((0, 8), (1, 32)), jnp.float32),
        "flux_y": noise(keys[2], (STEPS, NX, NY), 0.5, 3.0, ((0, 8), (1, 32)), jnp.float32),
        "source": noise(keys[3], (STEPS, NX, NY), 0.5, 3.0, ((0, 8), (1, 32)), jnp.float32),
        "potential": noise(keys[4], (STEPS, NX, NY), 1.0, 6.0, ((0, 8), (1, 32)), jnp.float32),
        "start_density": jnp.clip(0.2 + 1.8 * jax.random.uniform(keys[5], (NX, NY), jnp.float32) ** shard_levels(keys[5], (NX, NY), ((0, 32),), -0.2, 0.2), 0.2, 2.0),
        "end_density": jnp.clip(0.2 + 1.8 * jax.random.uniform(keys[6], (NX, NY), jnp.float32) ** shard_levels(keys[6], (NX, NY), ((0, 32),), -0.2, 0.2), 0.2, 2.0),
    }


tau_step = 0.04
sigma_step = 1.0
end_weight = 10.0


def proximal(moved_density, moved_flux_x, moved_flux_y, moved_source, scaling, target):
    energy = moved_flux_x * moved_flux_x + moved_flux_y * moved_flux_y + moved_source * moved_source
    root = jnp.maximum(target / scaling, 0.0)
    for repeat in range(NEWTON):
        offset_rho = root + tau_step
        residue = scaling * root - target - 0.5 * tau_step * energy / (offset_rho * offset_rho)
        derivative = scaling + tau_step * energy / (offset_rho * offset_rho * offset_rho)
        root = jnp.maximum(root - residue / derivative, 0.0)
    factor = root / (root + tau_step)
    return root, factor * moved_flux_x, factor * moved_flux_y, factor * moved_source


def reference(density, flux_x, flux_y, source, potential, start_density, end_density):
    steps_all = density.shape[0]
    local_time = lax.broadcasted_iota(jnp.int32, (steps_all, 1, 1), 0)
    at_end = local_time == steps_all - 1
    scaling = jnp.where(at_end, 1.0 + tau_step * end_weight, 1.0)
    attract = jnp.where(at_end, tau_step * end_weight, 0.0) * end_density[None]
    state_now = (density, flux_x, flux_y, source)
    extrap = state_now
    for repeat in range(ITERS):
        bar_rho, bar_fx, bar_fy, bar_src = extrap
        before_rho = jnp.concatenate([start_density[None], bar_rho[:-1]], 0)
        spread = bar_rho - before_rho + bar_fx - jnp.roll(bar_fx, 1, 1) + bar_fy - jnp.roll(bar_fy, 1, 2) - bar_src
        new_potential = potential + sigma_step * spread
        next_time = jnp.concatenate([new_potential[1:], jnp.zeros_like(new_potential[:1])], 0)
        next_row = jnp.roll(new_potential, -1, 1)
        next_column = jnp.roll(new_potential, -1, 2)
        moved_rho = state_now[0] - tau_step * (new_potential - next_time)
        moved_fx = state_now[1] - tau_step * (new_potential - next_row)
        moved_fy = state_now[2] - tau_step * (new_potential - next_column)
        moved_src = state_now[3] + tau_step * new_potential
        target = moved_rho + attract
        updated = proximal(moved_rho, moved_fx, moved_fy, moved_src, scaling, target)
        extrap = tuple(2.0 * fresh - older for fresh, older in zip(updated, state_now))
        state_now = updated
        potential = new_potential
    return state_now[0], state_now[1], state_now[2], state_now[3], potential
```

```python
import functools

import jax
import jax.numpy as jnp
from jax import lax
from jax.experimental import pallas as pl
from jax.experimental.pallas import tpu as pltpu
from jax.sharding import PartitionSpec as P

NEWTON = 8
ITERS = 6

tau_step = 0.04
end_weight = 10.0

T = 16
R = 16
PAIRS = T // 2
BLOCK = 8
TILE = (8, 128)
MESH = pl.DeviceIdType.MESH


def previous_column(x):
    moved = pltpu.roll(x, 1, 2)
    lane = lax.broadcasted_iota(jnp.int32, x.shape, 2)
    return jnp.where(lane == 0, pltpu.roll(moved, 1, 1), moved)


def next_column(x):
    moved = pltpu.roll(x, 127, 2)
    lane = lax.broadcasted_iota(jnp.int32, x.shape, 2)
    return jnp.where(lane == 127, pltpu.roll(moved, 7, 1), moved)


def newton(top, energy):
    twice = tau_step * energy
    thrice = (1.5 * tau_step) * energy
    q = jnp.maximum(top, tau_step)
    for repeat in range(NEWTON):
        square = q * q
        step = (top * square + thrice) / (square * q + twice)
        q = jnp.maximum(step * q, tau_step)
    root = q - tau_step
    return root, root / q


def kernel(
    sizes,
    rho_in, fx_in, fy_in, src_in, pot_in, start_in, end_in,
    rho_out, fx_out, fy_out, src_out, pot_out,
    raw, edge, pot, psi, bar_rho, bar_fx, rho, fx, fy, src, start, end,
    plane_out, fx_rows_out, pot_rows_out,
    rho_halo, pot_halo, fx_rows, pot_rows, fx_corner, rho_corner,
    in_sem, edge_sem, out_sem,
    plane_send, fx_send, pot_send,
    plane_recv, fx_recv, pot_recv,
):
    n_time, n_space = sizes
    me_time, me_space = lax.axis_index("tm"), lax.axis_index("space")
    time_next = lax.rem(me_time + 1, n_time)
    time_prev = lax.rem(me_time + n_time - 1, n_time)
    space_next = lax.rem(me_space + 1, n_space)
    space_prev = lax.rem(me_space + n_space - 1, n_space)
    first = me_time == 0
    last = me_time == n_time - 1

    fields_in = (rho_in, fx_in, fy_in, src_in, pot_in)
    fields_out = (rho_out, fx_out, fy_out, src_out, pot_out)
    plane_rows = R * 8

    def plane_in(n, t):
        rows = pl.ds(t * plane_rows, plane_rows)
        return pltpu.make_async_copy(fields_in[n].at[rows], raw.at[n, rows], in_sem.at[n, t])

    def plane_result(n, t):
        rows = pl.ds(t * plane_rows, plane_rows)
        return pltpu.make_async_copy(raw.at[n, rows], fields_out[n].at[rows], out_sem.at[n, t])

    def edge_in(n):
        return pltpu.make_async_copy((start_in, end_in)[n], edge.at[n], edge_sem.at[n])

    for n in range(2):
        edge_in(n).start()
    for u in range(PAIRS):
        for t in (u, T - 1 - u):
            for n in range(5):
                plane_in(n, t).start()

    barrier = pltpu.get_barrier_semaphore()
    partners = (
        (time_next, me_space), (time_prev, me_space),
        (me_time, space_next), (me_time, space_prev),
        (time_prev, space_next), (time_next, space_prev),
    )
    for partner in partners:
        pl.semaphore_signal(barrier, inc=1, device_id=partner, device_id_type=MESH)
    pl.semaphore_wait(barrier, len(partners))

    def send(source, target, send_sem, recv_sem, device):
        return pltpu.make_async_remote_copy(
            src_ref=source, dst_ref=target, send_sem=send_sem, recv_sem=recv_sem,
            device_id=device, device_id_type=MESH,
        )

    def send_rho(slot):
        return send(bar_rho.at[T - 1], rho_halo.at[slot], plane_send.at[0], plane_recv.at[slot, 0], (time_next, me_space))

    def send_pot(slot):
        return send(plane_out, pot_halo.at[slot], plane_send.at[1], plane_recv.at[slot, 1], (time_prev, me_space))

    def send_fx_corner(slot):
        return send(fx_rows_out.at[0], fx_corner.at[slot], plane_send.at[2], plane_recv.at[slot, 2], (time_prev, space_next))

    def send_rho_corner(slot):
        return send(bar_rho.at[T - 1, 0], rho_corner.at[slot], plane_send.at[3], plane_recv.at[slot, 3], (time_next, space_prev))

    def send_fx_rows(slot, u):
        rows = pl.ds(2 * u, 2)
        return send(fx_rows_out.at[rows], fx_rows.at[slot, rows], fx_send.at[u], fx_recv.at[slot, u], (me_time, space_next))

    def send_pot_rows(slot, u):
        rows = pl.ds(2 * u, 2)
        return send(pot_rows_out.at[rows], pot_rows.at[slot, rows], pot_send.at[u], pot_recv.at[slot, u], (me_time, space_prev))

    def send_pot_first(slot):
        rows = pl.ds(0, 1)
        return send(pot_rows_out.at[rows], pot_rows.at[slot, rows], pot_send.at[0], pot_recv.at[slot, 0], (me_time, space_prev))

    def send_pot_last(slot):
        rows = pl.ds(2 * PAIRS + 1, 1)
        return send(
            pot_rows_out.at[rows], pot_rows.at[slot, rows], pot_send.at[PAIRS], pot_recv.at[slot, PAIRS], (me_time, space_prev)
        )

    def emit_first(slot):
        plane_out[0] = pot[0, 0]
        plane_out[1:R] = pot[0, 1:R] - bar_fx[0, 0 : R - 1]
        fx_rows_out[0] = bar_fx[0, R - 1]
        fx_rows_out[1] = bar_fx[T - 1, R - 1]
        pot_rows_out[0] = pot[0, 0] - jnp.where(first, start[0], jnp.zeros(TILE, jnp.float32))
        send_pot(slot).start()
        send_rho(slot).start()
        send_fx_corner(slot).start()
        send_rho_corner(slot).start()
        send_fx_rows(slot, 0).start()
        send_pot_first(slot).start()

    def emit(slot, u):
        fx_rows_out[2 * u] = bar_fx[u, R - 1]
        fx_rows_out[2 * u + 1] = bar_fx[T - 1 - u, R - 1]
        pot_rows_out[2 * u] = pot[u, 0] - bar_rho[u - 1, 0]
        pot_rows_out[2 * u + 1] = pot[T - u, 0] - bar_rho[T - 1 - u, 0]
        send_fx_rows(slot, u).start()
        send_pot_rows(slot, u).start()

    def emit_last(slot):
        pot_rows_out[2 * PAIRS + 1] = pot[PAIRS, 0] - bar_rho[PAIRS - 1, 0]
        send_pot_last(slot).start()

    def divergence(b_rho, b_fx, b_fy, b_src):
        return b_rho + b_fx + (b_fy - previous_column(b_fy)) - b_src

    for n, ref in enumerate((start, end)):
        edge_in(n).wait()
        for i in range(R):
            ref[i] = edge[n, pl.ds((i // 8) * 64 + i % 8, 8, stride=8), :]

    def load_plane(t):
        for n in range(5):
            plane_in(n, t).wait()

        for i in range(R):
            rows = pl.ds(t * plane_rows + (i // 8) * 64 + i % 8, 8, stride=8)
            d, x, y, s, p = (raw[n, rows, :] for n in range(5))
            rho[t, i] = d
            fx[t, i] = x
            fy[t, i] = y
            src[t, i] = s
            bar_rho[t, i] = d
            bar_fx[t, i] = x
            pot[t, i] = p + divergence(d[None], x[None], y[None], s[None])[0]

    load_plane(0)
    load_plane(T - 1)
    emit_first(0)

    def load_pair(u, carry):
        load_plane(u)
        load_plane(T - 1 - u)
        emit(0, u)
        return carry

    lax.fori_loop(1, PAIRS, load_pair, 0)
    emit_last(0)

    def store_potential(t, new):
        pot[t] = new
        psi[t, 0:R] = tau_step * new

    def potential(t, slot, halo):
        below = bar_rho[t - 1]
        pot_0 = pot[t, 0] - below[0] - fx_rows[slot, halo]
        pot_n = pot[t, 1:R] - below[1:R] - bar_fx[t, 0 : R - 1]
        pot[t, 0] = pot_0
        pot[t, 1:R] = pot_n
        psi[t, 0] = tau_step * pot_0
        psi[t, 1:R] = tau_step * pot_n

    def update(t, final, end_scale=None, end_pull=None):
        for i0 in range(0, R, BLOCK):
            rows = pl.ds(i0, BLOCK)
            here = psi[t, rows]
            old = rho[t, rows], fx[t, rows], fy[t, rows], src[t, rows]
            target = old[0] - (here - psi[t + 1, rows])
            moved_fx = old[1] - (here - psi[t, pl.ds(i0 + 1, BLOCK)])
            moved_fy = old[2] - (here - next_column(here))
            moved_src = old[3] + here
            energy = moved_fx * moved_fx + moved_fy * moved_fy + moved_src * moved_src
            if end_scale is not None:
                target = (target + end_pull * end[rows]) * end_scale
                energy = energy * end_scale
            root, factor = newton(target + tau_step, energy)
            new = root, factor * moved_fx, factor * moved_fy, factor * moved_src
            if final:
                for n, value in enumerate(new + (pot[t, rows],)):
                    for i in range(BLOCK):
                        row = i0 + i
                        raw[n, pl.ds(t * plane_rows + (row // 8) * 64 + row % 8, 8, stride=8), :] = value[i]
            else:
                bars = tuple(fresh + (fresh - older) for fresh, older in zip(new, old))
                rho[t, rows], fx[t, rows], fy[t, rows], src[t, rows] = new
                pot[t, rows] = pot[t, rows] + divergence(*bars)
                bar_rho[t, rows] = bars[0]
                bar_fx[t, rows] = bars[1]

    def next_row_halo(t, slot, row, corner=None):
        value = pot_rows[slot, row] - bar_fx[t, R - 1]
        if corner is not None:
            value = value - corner
        psi[t, R] = tau_step * value

    def first_pair(now, later, final):
        send_fx_rows(now, 0).wait_recv()
        send_fx_rows(now, 1).wait_recv()
        send_rho(now).wait_recv()
        send_pot(now).wait_recv()
        send_fx_corner(now).wait_recv()
        before = jnp.where(first, start[...], rho_halo[now])
        pot_0 = pot[0, 0] - before[0] - fx_rows[now, 0]
        pot_n = pot[0, 1:R] - before[1:R] - bar_fx[0, 0 : R - 1]
        pot[0, 0] = pot_0
        pot[0, 1:R] = pot_n
        psi[0, 0] = tau_step * pot_0
        psi[0, 1:R] = tau_step * pot_n
        above = pot_halo[now] - bar_rho[T - 1]
        psi[T, 0:R] = jnp.where(last, jnp.zeros_like(above), tau_step * above)
        corner = psi[T, 0] - tau_step * fx_corner[now]
        psi[T, 0] = jnp.where(last, jnp.zeros_like(corner), corner)
        potential(1, now, 2)
        potential(T - 1, now, 1)
        send_pot_first(now).wait_recv()
        send_pot_rows(now, 1).wait_recv()
        send_rho_corner(now).wait_recv()
        next_row_halo(0, now, 0, jnp.where(first, jnp.zeros(TILE, jnp.float32), rho_corner[now]))
        next_row_halo(T - 1, now, 3)
        send_rho(now).wait_send()
        send_pot(now).wait_send()
        send_fx_corner(now).wait_send()
        send_rho_corner(now).wait_send()
        send_fx_rows(now, 0).wait_send()
        send_pot_first(now).wait_send()
        update(0, final)
        scale = jnp.where(last, 1.0 / (1.0 + tau_step * end_weight), 1.0).astype(jnp.float32)
        pull = jnp.where(last, tau_step * end_weight, 0.0).astype(jnp.float32)
        update(T - 1, final, scale, pull)
        if final:
            write_pair(0)
        else:
            emit_first(later)

    def write_pair(u):
        for t in (u, T - 1 - u):
            for n in range(5):
                plane_result(n, t).start()

    def middle_pair(u, now, later, final):
        @pl.when(u < PAIRS - 1)
        def _():
            send_fx_rows(now, u + 1).wait_recv()
            potential(u + 1, now, 2 * u + 2)
            send_pot_rows(now, u + 1).wait_recv()

        @pl.when(u == PAIRS - 1)
        def _():
            send_pot_last(now).wait_recv()

        potential(T - 1 - u, now, 2 * u + 1)
        next_row_halo(u, now, 2 * u)
        next_row_halo(T - 1 - u, now, 2 * u + 3)
        send_fx_rows(now, u).wait_send()
        send_pot_rows(now, u).wait_send()
        update(u, final)
        update(T - 1 - u, final)
        if final:
            write_pair(u)
        else:
            emit(later, u)

    def iteration(now, later, final):
        first_pair(now, later, final)

        def pair(u, carry):
            middle_pair(u, now, later, final)
            return carry

        lax.fori_loop(1, PAIRS, pair, 0)
        send_pot_last(now).wait_send()
        if not final:
            emit_last(later)

    def step(k, carry):
        iteration(lax.rem(k - 1, 2), lax.rem(k, 2), False)
        return carry

    lax.fori_loop(1, ITERS, step, 0)
    iteration((ITERS - 1) % 2, None, True)

    for t in range(T):
        for n in range(5):
            plane_result(n, t).wait()


def to_rows(x):
    planes = x.shape[0]
    return x.reshape(planes, R // 8, 8, 8, 128).transpose(0, 1, 3, 2, 4).reshape(planes * R * 8, 128)


def from_rows(x):
    return x.reshape(T, R // 8, 8, 8, 128).transpose(0, 1, 3, 2, 4).reshape(T, R, 1024)


def solution(mesh):
    sizes = mesh.shape["tm"], mesh.shape["space"]
    f32 = jnp.float32
    vmem = pltpu.VMEM
    dma = pltpu.SemaphoreType.DMA

    def body(density, flux_x, flux_y, source, potential, start_density, end_density):
        anywhere = pl.BlockSpec(memory_space=pl.ANY)
        rows = T * R * 8
        results = pl.pallas_call(
            functools.partial(kernel, sizes),
            out_shape=[jax.ShapeDtypeStruct((rows, 128), f32)] * 5,
            in_specs=[anywhere] * 7,
            out_specs=[anywhere] * 5,
            scratch_shapes=[
                vmem((5, rows, 128), f32),
                vmem((2, R * 8, 128), f32),
                vmem((T, R) + TILE, f32),
                vmem((T + 1, R + 1) + TILE, f32),
                vmem((T, R) + TILE, f32),
                vmem((T, R) + TILE, f32),
                vmem((T, R) + TILE, f32),
                vmem((T, R) + TILE, f32),
                vmem((T, R) + TILE, f32),
                vmem((T, R) + TILE, f32),
                vmem((R,) + TILE, f32),
                vmem((R,) + TILE, f32),
                vmem((R,) + TILE, f32),
                vmem((2 * PAIRS,) + TILE, f32),
                vmem((2 * PAIRS + 2,) + TILE, f32),
                vmem((2, R) + TILE, f32),
                vmem((2, R) + TILE, f32),
                vmem((2, 2 * PAIRS) + TILE, f32),
                vmem((2, 2 * PAIRS + 2) + TILE, f32),
                vmem((2,) + TILE, f32),
                vmem((2,) + TILE, f32),
                dma((5, T)),
                dma((2,)),
                dma((5, T)),
                dma((4,)),
                dma((PAIRS,)),
                dma((PAIRS + 1,)),
                dma((2, 4)),
                dma((2, PAIRS)),
                dma((2, PAIRS + 1)),
            ],
            compiler_params=pltpu.CompilerParams(collective_id=0, has_side_effects=True),
        )(
            *(to_rows(x) for x in (density, flux_x, flux_y, source, potential)),
            to_rows(start_density[None]),
            to_rows(end_density[None]),
        )
        return tuple(from_rows(x) for x in results)

    volume, plane = P("tm", "space", None), P("space", None)
    return jax.shard_map(
        body, mesh=mesh, in_specs=(volume,) * 5 + (plane,) * 2, out_specs=(volume,) * 5, check_vma=False
    )
```

```python
import collections
import functools

import jax
import jax.numpy as jnp
from jax import lax
from jax.experimental import pallas as pl
from jax.experimental.pallas import tpu as pltpu
from jax.sharding import PartitionSpec as P

NEWTON = 8
ITERS = 6

tau_step = 0.04
end_weight = 10.0

T = 16
R = 16
PAIRS = T // 2
TILE = (8, 128)
MESH = pl.DeviceIdType.MESH


Half = collections.namedtuple("Half", ("rho", "fx", "fy", "src", "part", "pot", "psi"))


def previous_column(x):
    moved = pltpu.roll(x, 1, 2)
    lane = lax.broadcasted_iota(jnp.int32, x.shape, 2)
    return jnp.where(lane == 0, pltpu.roll(moved, 1, 1), moved)


def next_column(x):
    moved = pltpu.roll(x, 127, 2)
    lane = lax.broadcasted_iota(jnp.int32, x.shape, 2)
    return jnp.where(lane == 127, pltpu.roll(moved, 7, 1), moved)


unit = 1.0 / tau_step


def newton(top, energy):
    half = 0.5 * energy
    thrice = energy + half
    q = jnp.maximum(top, 1.0)
    top = jnp.maximum(top, 1.0 - half)
    for repeat in range(NEWTON):
        square = q * q
        q = (top * square + thrice) / (square * q + energy) * q
    q = jnp.maximum(q, 1.0)
    return q, (q - 1.0) / q


def kernel(
    sizes,
    rho_in, fx_in, fy_in, src_in, pot_in, start_in, end_in,
    rho_out, fx_out, fy_out, src_out, pot_out,
    raw, edge, lower_refs, upper_refs, start, end,
    plane_out, fx_rows_out, pot_rows_out,
    rho_halo, pot_halo, fx_rows, pot_rows, fx_corner, rho_corner,
    in_sem, edge_sem,
    plane_send, fx_send, pot_send,
    plane_recv, fx_recv, pot_recv,
):
    lower, upper = Half(*lower_refs), Half(*upper_refs)
    n_time, n_space = sizes
    me_time, me_space = lax.axis_index("tm"), lax.axis_index("space")
    time_next = lax.rem(me_time + 1, n_time)
    time_prev = lax.rem(me_time + n_time - 1, n_time)
    space_next = lax.rem(me_space + 1, n_space)
    space_prev = lax.rem(me_space + n_space - 1, n_space)
    first = me_time == 0
    last = me_time == n_time - 1

    fields_in = (rho_in, fx_in, fy_in, src_in, pot_in)
    fields_out = (rho_out, fx_out, fy_out, src_out, pot_out)
    plane_rows = R * 8

    def plane_in(n, t):
        rows = pl.ds(t * plane_rows, plane_rows)
        return pltpu.make_async_copy(fields_in[n].at[rows], raw.at[n, rows], in_sem.at[n, t])

    def edge_in(n):
        return pltpu.make_async_copy((start_in, end_in)[n], edge.at[n], edge_sem.at[n])

    barrier = pltpu.get_barrier_semaphore()
    partners = (
        (time_next, me_space), (time_prev, me_space),
        (me_time, space_next), (me_time, space_prev),
        (time_prev, space_next), (time_next, space_prev),
    )
    for partner in partners:
        pl.semaphore_signal(barrier, inc=1, device_id=partner, device_id_type=MESH)

    for u in range(PAIRS):
        for t in (u, T - 1 - u):
            for n in range(5):
                plane_in(n, t).start()
        if u == 0:
            for n in range(2):
                edge_in(n).start()

    def send(source, target, send_sem, recv_sem, device):
        return pltpu.make_async_remote_copy(
            src_ref=source, dst_ref=target, send_sem=send_sem, recv_sem=recv_sem,
            device_id=device, device_id_type=MESH,
        )

    def send_rho(slot):
        return send(upper.rho.at[0], rho_halo.at[slot], plane_send.at[0], plane_recv.at[slot, 0], (time_next, me_space))

    def send_pot(slot):
        return send(plane_out, pot_halo.at[slot], plane_send.at[1], plane_recv.at[slot, 1], (time_prev, me_space))

    def send_fx_corner(slot):
        return send(fx_rows_out.at[0], fx_corner.at[slot], plane_send.at[2], plane_recv.at[slot, 2], (time_prev, space_next))

    def send_rho_corner(slot):
        return send(upper.rho.at[0, 0], rho_corner.at[slot], plane_send.at[3], plane_recv.at[slot, 3], (time_next, space_prev))

    def send_fx_rows(slot, u):
        rows = pl.ds(2 * u, 2)
        return send(fx_rows_out.at[rows], fx_rows.at[slot, rows], fx_send.at[u], fx_recv.at[slot, u], (me_time, space_next))

    def send_pot_rows(slot, u):
        rows = pl.ds(2 * u, 2)
        return send(pot_rows_out.at[rows], pot_rows.at[slot, rows], pot_send.at[u], pot_recv.at[slot, u], (me_time, space_prev))

    def send_pot_first(slot):
        rows = pl.ds(0, 1)
        return send(pot_rows_out.at[rows], pot_rows.at[slot, rows], pot_send.at[0], pot_recv.at[slot, 0], (me_time, space_prev))

    def send_pot_last(slot):
        rows = pl.ds(2 * PAIRS + 1, 1)
        return send(
            pot_rows_out.at[rows], pot_rows.at[slot, rows], pot_send.at[PAIRS], pot_recv.at[slot, PAIRS], (me_time, space_prev)
        )

    def emit_first(slot, gain):
        part, pot, fx = lower.part, lower.pot, lower.fx
        plane_out[0] = pot[0, 0] + gain * part[0, 0]
        plane_out[1:R] = pot[0, 1:R] + gain * (part[0, 1:R] - fx[0, 0 : R - 1])
        fx_rows_out[0] = fx[0, R - 1]
        fx_rows_out[1] = upper.fx[0, R - 1]
        held = jnp.where(first, start[0], jnp.zeros(TILE, jnp.float32))
        pot_rows_out[0] = pot[0, 0] + gain * (part[0, 0] - held)
        send_fx_corner(slot).start()
        send_rho_corner(slot).start()
        send_fx_rows(slot, 0).start()
        send_pot_first(slot).start()
        send_pot(slot).start()
        send_rho(slot).start()

    def emit(slot, u, gain):
        fx_rows_out[2 * u] = lower.fx[u, R - 1]
        fx_rows_out[2 * u + 1] = upper.fx[u, R - 1]
        pot_rows_out[2 * u] = lower.pot[u, 0] + gain * (lower.part[u, 0] - lower.rho[u - 1, 0])
        pot_rows_out[2 * u + 1] = upper.pot[u - 1, 0] + gain * (upper.part[u - 1, 0] - upper.rho[u, 0])
        send_fx_rows(slot, u).start()
        send_pot_rows(slot, u).start()

    def emit_last(slot, gain):
        u = PAIRS - 1
        pot_rows_out[2 * PAIRS + 1] = upper.pot[u, 0] + gain * (upper.part[u, 0] - lower.rho[u, 0])
        send_pot_last(slot).start()

    for n, ref in enumerate((start, end)):
        edge_in(n).wait()
        for i in range(R):
            value = edge[n, pl.ds((i // 8) * 64 + i % 8, 8, stride=8), :]
            ref[i] = value * unit + (1.0 if n == 0 else 0.0)

    def load_plane(t, half, u):
        for n in range(5):
            plane_in(n, t).wait()
        for i in range(R):
            rows = pl.ds(t * plane_rows + (i // 8) * 64 + i % 8, 8, stride=8)
            d, x, y, s, p = (unit * raw[n, rows, :] for n in range(5))
            d = d + 1.0
            half.rho[u, i] = d
            half.fx[u, i] = x
            half.fy[u, i] = y
            half.src[u, i] = s
            half.pot[u, i] = p
            half.part[u, i] = d + x + (y - previous_column(y[None])[0]) - s

    load_plane(0, lower, 0)
    load_plane(T - 1, upper, 0)
    pl.semaphore_wait(barrier, len(partners))
    emit_first(0, 1.0)

    def load_pair(u, carry):
        load_plane(u, lower, u)
        load_plane(T - 1 - u, upper, u)
        emit(0, u, 1.0)
        return carry

    lax.fori_loop(1, PAIRS, load_pair, 0)
    emit_last(0, 1.0)

    def potential(half, u, keep, below, row):
        beside = jnp.concatenate([row[None], half.fx[u, 0 : R - 1]], 0)
        gap = half.part[u] - (below + beside)
        base = half.pot[u] + keep * gap
        half.pot[u] = base
        new = tau_step * (base + gap)
        half.psi[u] = new
        return new

    def update(half, u, t, final, here, above, row, end_scale=None, end_pull=None):
        top = half.rho[u] - (here - above)
        moved_fx = half.fx[u] - (here - jnp.concatenate([here[1:R], row[None]], 0))
        moved_fy = half.fy[u] - (here - next_column(here))
        moved_src = half.src[u] + here
        energy = moved_fx * moved_fx + moved_fy * moved_fy + moved_src * moved_src
        if end_scale is not None:
            top = (top - 1.0 + end_pull * end[...]) * end_scale + 1.0
            energy = energy * end_scale
        q, factor = newton(top, energy)
        new_fx, new_fy, new_src = factor * moved_fx, factor * moved_fy, factor * moved_src
        if final:
            results = tau_step * (q - 1.0), tau_step * new_fx, tau_step * new_fy, tau_step * new_src, here
            for ref, value in zip((rho_out, fx_out, fy_out, src_out, pot_out), results):
                for i in range(R):
                    ref[pl.ds(t * plane_rows + (i // 8) * 64 + i % 8, 8, stride=8), :] = value[i]
        else:
            half.rho[u], half.fx[u], half.fy[u], half.src[u] = q, new_fx, new_fy, new_src
            half.part[u] = q + new_fx + (new_fy - previous_column(new_fy)) - new_src

    def halo_row(half, u, slot, row, gain, corner=None):
        held = half.fx[u, R - 1]
        if corner is not None:
            held = held + corner
        return tau_step * (pot_rows[slot, row] - gain * held)

    def first_pair(now, later, gain, final):
        keep = gain - 1.0
        send_fx_rows(now, 0).wait_recv()
        send_fx_rows(now, 1).wait_recv()
        send_rho(now).wait_recv()
        send_pot(now).wait_recv()
        send_fx_corner(now).wait_recv()
        send_pot_first(now).wait_recv()
        send_pot_rows(now, 1).wait_recv()
        send_rho_corner(now).wait_recv()
        send_rho(now).wait_send()
        send_pot(now).wait_send()
        send_fx_corner(now).wait_send()
        send_rho_corner(now).wait_send()
        send_fx_rows(now, 0).wait_send()
        send_pot_first(now).wait_send()
        lower_row = halo_row(lower, 0, now, 0, gain, jnp.where(first, jnp.zeros(TILE, jnp.float32), rho_corner[now]))
        upper_row = halo_row(upper, 0, now, 3, gain)
        scale = jnp.where(last, 1.0 / (1.0 + tau_step * end_weight), 1.0).astype(jnp.float32)
        pull = jnp.where(last, tau_step * end_weight, 0.0).astype(jnp.float32)
        above = tau_step * (pot_halo[now] - gain * upper.rho[0])
        above = jnp.concatenate([above[0:1] - (tau_step * (gain * fx_corner[now]))[None], above[1:R]], 0)
        above = jnp.where(last, jnp.zeros_like(above), above)
        before = jnp.where(first, start[...], rho_halo[now])
        lower_here = potential(lower, 0, keep, before, fx_rows[now, 0])
        lower_above = potential(lower, 1, keep, lower.rho[0], fx_rows[now, 2])
        upper_here = potential(upper, 0, keep, upper.rho[1], fx_rows[now, 1])
        update(lower, 0, 0, final, lower_here, lower_above, lower_row)
        update(upper, 0, T - 1, final, upper_here, above, upper_row, scale, pull)
        if not final:
            emit_first(later, 2.0)

    def middle_pair(u, now, later, gain, final, meet):
        keep = gain - 1.0
        if meet:
            send_pot_last(now).wait_recv()
        else:
            send_fx_rows(now, u + 1).wait_recv()
            send_pot_rows(now, u + 1).wait_recv()
        send_fx_rows(now, u).wait_send()
        send_pot_rows(now, u).wait_send()
        lower_row = halo_row(lower, u, now, 2 * u, gain)
        upper_row = halo_row(upper, u, now, 2 * u + 3, gain)
        upper_below = lower.rho[u] if meet else upper.rho[u + 1]
        upper_here = potential(upper, u, keep, upper_below, fx_rows[now, 2 * u + 1])
        lower_above = upper_here if meet else potential(lower, u + 1, keep, lower.rho[u], fx_rows[now, 2 * u + 2])
        lower_here, upper_above = lower.psi[u], upper.psi[u - 1]
        update(lower, u, u, final, lower_here, lower_above, lower_row)
        update(upper, u, T - 1 - u, final, upper_here, upper_above, upper_row)
        if not final:
            emit(later, u, 2.0)

    def iteration(now, later, gain, final):
        first_pair(now, later, gain, final)

        def pair(u, carry):
            middle_pair(u, now, later, gain, final, False)
            return carry

        lax.fori_loop(1, PAIRS - 1, pair, 0)
        middle_pair(PAIRS - 1, now, later, gain, final, True)
        send_pot_last(now).wait_send()
        if not final:
            emit_last(later, 2.0)

    def step(k, carry):
        gain = jnp.where(k == 1, 1.0, 2.0).astype(jnp.float32)
        iteration(lax.rem(k - 1, 2), lax.rem(k, 2), gain, False)
        return carry

    lax.fori_loop(1, ITERS, step, 0)
    iteration((ITERS - 1) % 2, None, 2.0, True)


def write_kernel(*refs):
    results, targets, sem = refs[:5], refs[5:10], refs[10]
    for n in range(5):
        pltpu.make_async_copy(results[n], targets[n], sem.at[n]).start()
    for n in range(5):
        pltpu.make_async_copy(results[n], targets[n], sem.at[n]).wait()


def to_rows(x):
    planes = x.shape[0]
    return x.reshape(planes, R // 8, 8, 8, 128).transpose(0, 1, 3, 2, 4).reshape(planes * R * 8, 128)


def in_hbm(x):
    return pltpu.with_memory_space_constraint(x, pltpu.HBM)


def from_rows(x):
    return x.reshape(T, R // 8, 8, 8, 128).transpose(0, 1, 3, 2, 4).reshape(T, R, 1024)


def solution(mesh):
    sizes = mesh.shape["tm"], mesh.shape["space"]
    f32 = jnp.float32
    vmem = pltpu.VMEM
    dma = pltpu.SemaphoreType.DMA

    def body(density, flux_x, flux_y, source, potential, start_density, end_density):
        anywhere = pl.BlockSpec(memory_space=pltpu.HBM)
        on_chip = pl.BlockSpec(memory_space=vmem)
        rows = T * R * 8
        results = pl.pallas_call(
            functools.partial(kernel, sizes),
            out_shape=[vmem((rows, 128), f32)] * 5,
            in_specs=[anywhere] * 7,
            out_specs=[on_chip] * 5,
            scratch_shapes=[
                vmem((5, rows, 128), f32),
                vmem((2, R * 8, 128), f32),
                [vmem((PAIRS, R) + TILE, f32)] * 7,
                [vmem((PAIRS, R) + TILE, f32)] * 7,
                vmem((R,) + TILE, f32),
                vmem((R,) + TILE, f32),
                vmem((R,) + TILE, f32),
                vmem((2 * PAIRS,) + TILE, f32),
                vmem((2 * PAIRS + 2,) + TILE, f32),
                vmem((2, R) + TILE, f32),
                vmem((2, R) + TILE, f32),
                vmem((2, 2 * PAIRS) + TILE, f32),
                vmem((2, 2 * PAIRS + 2) + TILE, f32),
                vmem((2,) + TILE, f32),
                vmem((2,) + TILE, f32),
                dma((5, T)),
                dma((2,)),
                dma((4,)),
                dma((PAIRS,)),
                dma((PAIRS + 1,)),
                dma((2, 4)),
                dma((2, PAIRS)),
                dma((2, PAIRS + 1)),
            ],
            compiler_params=pltpu.CompilerParams(
                collective_id=0, has_side_effects=True, vmem_limit_bytes=24 << 20
            ),
        )(
            *(in_hbm(to_rows(x)) for x in (density, flux_x, flux_y, source, potential)),
            in_hbm(to_rows(start_density[None])),
            in_hbm(to_rows(end_density[None])),
        )
        results = pl.pallas_call(
            write_kernel,
            out_shape=[jax.ShapeDtypeStruct((rows, 128), f32)] * 5,
            in_specs=[on_chip] * 5,
            out_specs=[anywhere] * 5,
            scratch_shapes=[dma((5,))],
            compiler_params=pltpu.CompilerParams(vmem_limit_bytes=1 << 20),
        )(*results)
        return tuple(from_rows(x) for x in results)

    volume, plane = P("tm", "space", None), P("space", None)
    return jax.shard_map(
        body, mesh=mesh, in_specs=(volume,) * 5 + (plane,) * 2, out_specs=(volume,) * 5, check_vma=False
    )
```

```python
import collections
import functools

import jax
import jax.numpy as jnp
from jax import lax
from jax.experimental import pallas as pl
from jax.experimental.pallas import tpu as pltpu
from jax.sharding import PartitionSpec as P

NEWTON = 8
ITERS = 6

tau_step = 0.04
end_weight = 10.0

T = 16
R = 16
PAIRS = T // 2
TOP, BOTTOM = 4, 12
OUTER, INNER = ((0, TOP), (BOTTOM, R)), ((TOP, BOTTOM),)
RHO_PARTS = (0, TOP), (BOTTOM, R), (TOP, TOP + 1), (TOP + 1, BOTTOM)
POT_PARTS = (0, TOP), (BOTTOM + 1, R), (BOTTOM, BOTTOM + 1), (TOP, BOTTOM)
TILE = (8, 128)
MESH = pl.DeviceIdType.MESH


Half = collections.namedtuple("Half", ("rho", "fx", "fy", "src", "part", "pot", "psi"))


def take(ref, u, parts):
    values = [ref[u, a:b] for a, b in parts]
    return values[0] if len(values) == 1 else jnp.concatenate(values, 0)


def put(ref, u, parts, value):
    done = 0
    for a, b in parts:
        ref[u, a:b] = value[done : done + b - a]
        done += b - a


def previous_column(x):
    moved = pltpu.roll(x, 1, 2)
    lane = lax.broadcasted_iota(jnp.int32, x.shape, 2)
    return jnp.where(lane == 0, pltpu.roll(moved, 1, 1), moved)


def next_column(x):
    moved = pltpu.roll(x, 127, 2)
    lane = lax.broadcasted_iota(jnp.int32, x.shape, 2)
    return jnp.where(lane == 127, pltpu.roll(moved, 7, 1), moved)


unit = 1.0 / tau_step


def newton(top, energy):
    half = 0.5 * energy
    thrice = energy + half
    q = jnp.maximum(top, 1.0)
    top = jnp.maximum(top, 1.0 - half)
    for repeat in range(NEWTON):
        square = q * q
        q = (top * square + thrice) / (square * q + energy) * q
    q = jnp.maximum(q, 1.0)
    return q, (q - 1.0) / q


def kernel(
    sizes,
    rho_in, fx_in, fy_in, src_in, pot_in, start_in, end_in,
    rho_out, fx_out, fy_out, src_out, pot_out,
    raw, edge, lower_refs, upper_refs, start, end,
    plane_out, fx_rows_out, pot_rows_out,
    rho_halo, pot_halo, fx_rows, pot_rows, fx_corner, rho_corner,
    in_sem, edge_sem,
    plane_send, fx_send, pot_send,
    plane_recv, fx_recv, pot_recv,
):
    lower, upper = Half(*lower_refs), Half(*upper_refs)
    n_time, n_space = sizes
    me_time, me_space = lax.axis_index("tm"), lax.axis_index("space")
    time_next = lax.rem(me_time + 1, n_time)
    time_prev = lax.rem(me_time + n_time - 1, n_time)
    space_next = lax.rem(me_space + 1, n_space)
    space_prev = lax.rem(me_space + n_space - 1, n_space)
    first = me_time == 0
    last = me_time == n_time - 1

    fields_in = (rho_in, fx_in, fy_in, src_in, pot_in)
    fields_out = (rho_out, fx_out, fy_out, src_out, pot_out)
    plane_rows = R * 8

    def plane_in(n, t):
        rows = pl.ds(t * plane_rows, plane_rows)
        return pltpu.make_async_copy(fields_in[n].at[rows], raw.at[n, rows], in_sem.at[n, t])

    def edge_in(n):
        return pltpu.make_async_copy((start_in, end_in)[n], edge.at[n], edge_sem.at[n])

    barrier = pltpu.get_barrier_semaphore()
    partners = (
        (time_next, me_space), (time_prev, me_space),
        (me_time, space_next), (me_time, space_prev),
        (time_prev, space_next), (time_next, space_prev),
    )
    for partner in partners:
        pl.semaphore_signal(barrier, inc=1, device_id=partner, device_id_type=MESH)

    for u in range(PAIRS):
        for t in (u, T - 1 - u):
            for n in range(5):
                plane_in(n, t).start()
        if u == 0:
            for n in range(2):
                edge_in(n).start()

    def send(source, target, send_sem, recv_sem, device):
        return pltpu.make_async_remote_copy(
            src_ref=source, dst_ref=target, send_sem=send_sem, recv_sem=recv_sem,
            device_id=device, device_id_type=MESH,
        )

    def send_rho(slot, n):
        a, b = RHO_PARTS[n]
        rows = pl.ds(a, b - a)
        return send(
            upper.rho.at[0, rows], rho_halo.at[slot, rows], plane_send.at[n], plane_recv.at[slot, n], (time_next, me_space)
        )

    def send_pot(slot, n):
        a, b = POT_PARTS[n]
        rows = pl.ds(a, b - a)
        return send(
            plane_out.at[rows], pot_halo.at[slot, rows], plane_send.at[4 + n], plane_recv.at[slot, 4 + n], (time_prev, me_space)
        )

    def send_fx_corner(slot):
        return send(fx_rows_out.at[0], fx_corner.at[slot], plane_send.at[8], plane_recv.at[slot, 8], (time_prev, space_next))

    def send_rho_corner(slot):
        return send(upper.rho.at[0, 0], rho_corner.at[slot], plane_send.at[9], plane_recv.at[slot, 9], (time_next, space_prev))

    def send_fx_rows(slot, u):
        rows = pl.ds(2 * u, 2)
        return send(fx_rows_out.at[rows], fx_rows.at[slot, rows], fx_send.at[u], fx_recv.at[slot, u], (me_time, space_next))

    def send_pot_rows(slot, u):
        rows = pl.ds(2 * u, 2)
        return send(pot_rows_out.at[rows], pot_rows.at[slot, rows], pot_send.at[u], pot_recv.at[slot, u], (me_time, space_prev))

    def send_pot_first(slot):
        rows = pl.ds(0, 1)
        return send(pot_rows_out.at[rows], pot_rows.at[slot, rows], pot_send.at[0], pot_recv.at[slot, 0], (me_time, space_prev))

    def send_pot_last(slot):
        rows = pl.ds(2 * PAIRS + 1, 1)
        return send(
            pot_rows_out.at[rows], pot_rows.at[slot, rows], pot_send.at[PAIRS], pot_recv.at[slot, PAIRS], (me_time, space_prev)
        )

    def emit_outer(slot, gain):
        part, pot, fx = lower.part, lower.pot, lower.fx
        fx_rows_out[0] = fx[0, R - 1]
        fx_rows_out[1] = upper.fx[0, R - 1]
        held = jnp.where(first, start[0], jnp.zeros(TILE, jnp.float32))
        pot_rows_out[0] = pot[0, 0] + gain * (part[0, 0] - held)
        plane_out[0] = pot[0, 0] + gain * part[0, 0]
        for a, b in ((1, TOP), (BOTTOM + 1, R)):
            plane_out[a:b] = pot[0, a:b] + gain * (part[0, a:b] - fx[0, a - 1 : b - 1])
        send_fx_corner(slot).start()
        send_rho_corner(slot).start()
        send_fx_rows(slot, 0).start()
        send_pot_first(slot).start()
        for n in (0, 1):
            send_pot(slot, n).start()
            send_rho(slot, n).start()

    def emit_inner(slot, gain):
        part, pot, fx = lower.part, lower.pot, lower.fx
        a, b = TOP, BOTTOM + 1
        plane_out[a:b] = pot[0, a:b] + gain * (part[0, a:b] - fx[0, a - 1 : b - 1])
        for n in (2, 3):
            send_pot(slot, n).start()
            send_rho(slot, n).start()

    def emit(slot, u, gain):
        fx_rows_out[2 * u] = lower.fx[u, R - 1]
        fx_rows_out[2 * u + 1] = upper.fx[u, R - 1]
        pot_rows_out[2 * u] = lower.pot[u, 0] + gain * (lower.part[u, 0] - lower.rho[u - 1, 0])
        pot_rows_out[2 * u + 1] = upper.pot[u - 1, 0] + gain * (upper.part[u - 1, 0] - upper.rho[u, 0])
        send_fx_rows(slot, u).start()
        send_pot_rows(slot, u).start()

    def emit_last(slot, gain):
        u = PAIRS - 1
        pot_rows_out[2 * PAIRS + 1] = upper.pot[u, 0] + gain * (upper.part[u, 0] - lower.rho[u, 0])
        send_pot_last(slot).start()

    for n, ref in enumerate((start, end)):
        edge_in(n).wait()
        for i in range(R):
            value = edge[n, pl.ds((i // 8) * 64 + i % 8, 8, stride=8), :]
            ref[i] = value * unit + (1.0 if n == 0 else 0.0)

    def load_plane(t, half, u):
        for n in range(5):
            plane_in(n, t).wait()
        for i in range(R):
            rows = pl.ds(t * plane_rows + (i // 8) * 64 + i % 8, 8, stride=8)
            d, x, y, s, p = (unit * raw[n, rows, :] for n in range(5))
            d = d + 1.0
            half.rho[u, i] = d
            half.fx[u, i] = x
            half.fy[u, i] = y
            half.src[u, i] = s
            half.pot[u, i] = p
            half.part[u, i] = d + x + (y - previous_column(y[None])[0]) - s

    load_plane(0, lower, 0)
    load_plane(T - 1, upper, 0)
    pl.semaphore_wait(barrier, len(partners))
    emit_outer(0, 1.0)
    emit_inner(0, 1.0)

    def load_pair(u, carry):
        load_plane(u, lower, u)
        load_plane(T - 1 - u, upper, u)
        emit(0, u, 1.0)
        return carry

    lax.fori_loop(1, PAIRS, load_pair, 0)
    emit_last(0, 1.0)

    def potential(half, u, keep, below, row, a=0, b=R):
        if a == 0:
            beside = jnp.concatenate([row[None], half.fx[u, 0 : b - 1]], 0)
        else:
            beside = half.fx[u, a - 1 : b - 1]
        gap = half.part[u, a:b] - (below + beside)
        base = half.pot[u, a:b] + keep * gap
        half.pot[u, a:b] = base
        new = tau_step * (base + gap)
        half.psi[u, a:b] = new
        return new

    def update(half, u, t, final, parts, here, above, after, end_scale=None, end_pull=None):
        top = take(half.rho, u, parts) - (here - above)
        moved_fx = take(half.fx, u, parts) - (here - after)
        moved_fy = take(half.fy, u, parts) - (here - next_column(here))
        moved_src = take(half.src, u, parts) + here
        energy = moved_fx * moved_fx + moved_fy * moved_fy + moved_src * moved_src
        if end_scale is not None:
            ends = jnp.concatenate([end[a:b] for a, b in parts], 0)
            top = (top - 1.0 + end_pull * ends) * end_scale + 1.0
            energy = energy * end_scale
        q, factor = newton(top, energy)
        new_fx, new_fy, new_src = factor * moved_fx, factor * moved_fy, factor * moved_src
        if final:
            results = tau_step * (q - 1.0), tau_step * new_fx, tau_step * new_fy, tau_step * new_src, here
            numbers = [i for a, b in parts for i in range(a, b)]
            for ref, value in zip((rho_out, fx_out, fy_out, src_out, pot_out), results):
                for n, i in enumerate(numbers):
                    ref[pl.ds(t * plane_rows + (i // 8) * 64 + i % 8, 8, stride=8), :] = value[n]
        else:
            new_part = q + new_fx + (new_fy - previous_column(new_fy)) - new_src
            for ref, value in zip(half[:5], (q, new_fx, new_fy, new_src, new_part)):
                put(ref, u, parts, value)

    def halo_row(half, u, slot, row, gain, corner=None):
        held = half.fx[u, R - 1]
        if corner is not None:
            held = held + corner
        return tau_step * (pot_rows[slot, row] - gain * held)

    def before(now, a, b):
        return jnp.where(first, start[a:b], rho_halo[now, a:b])

    def plane_above(now, gain, a, b):
        value = tau_step * (pot_halo[now, a:b] - gain * upper.rho[0, a:b])
        if a == 0:
            corner = tau_step * (gain * fx_corner[now])
            value = jnp.concatenate([value[0:1] - corner[None], value[1:]], 0)
        return jnp.where(last, jnp.zeros_like(value), value)

    end_scale = jnp.where(last, 1.0 / (1.0 + tau_step * end_weight), 1.0).astype(jnp.float32)
    end_pull = jnp.where(last, tau_step * end_weight, 0.0).astype(jnp.float32)

    def outer_rows(now, later, gain, final):
        keep = gain - 1.0
        send_fx_rows(now, 0).wait_recv()
        send_fx_rows(now, 1).wait_recv()
        send_fx_corner(now).wait_recv()
        send_pot_first(now).wait_recv()
        send_pot_rows(now, 1).wait_recv()
        send_rho_corner(now).wait_recv()
        for n in (0, 1, 2):
            send_rho(now, n).wait_recv()
            send_pot(now, n).wait_recv()
        for n in (0, 1):
            send_rho(now, n).wait_send()
            send_pot(now, n).wait_send()
        send_fx_corner(now).wait_send()
        send_rho_corner(now).wait_send()
        send_fx_rows(now, 0).wait_send()
        send_pot_first(now).wait_send()
        lower_row = halo_row(lower, 0, now, 0, gain, jnp.where(first, jnp.zeros(TILE, jnp.float32), rho_corner[now]))
        upper_row = halo_row(upper, 0, now, 3, gain)
        lower_above = potential(lower, 1, keep, lower.rho[0], fx_rows[now, 2])
        upper_here = potential(upper, 0, keep, upper.rho[1], fx_rows[now, 1])
        over = potential(lower, 0, keep, before(now, 0, TOP + 1), fx_rows[now, 0], 0, TOP + 1)
        under = potential(lower, 0, keep, before(now, BOTTOM, R), None, BOTTOM, R)
        here = jnp.concatenate([over[0:TOP], under], 0)
        after = jnp.concatenate([over[1 : TOP + 1], under[1:], lower_row[None]], 0)
        above = jnp.concatenate([lower_above[0:TOP], lower_above[BOTTOM:R]], 0)
        update(lower, 0, 0, final, OUTER, here, above, after)
        here = jnp.concatenate([upper_here[0:TOP], upper_here[BOTTOM:R]], 0)
        after = jnp.concatenate([upper_here[1 : TOP + 1], upper_here[BOTTOM + 1 : R], upper_row[None]], 0)
        above = jnp.concatenate([plane_above(now, gain, 0, TOP), plane_above(now, gain, BOTTOM, R)], 0)
        update(upper, 0, T - 1, final, OUTER, here, above, after, end_scale, end_pull)
        if not final:
            emit_outer(later, 2.0)

    def inner_rows(now, later, gain, final):
        send_rho(now, 3).wait_recv()
        send_pot(now, 3).wait_recv()
        for n in (2, 3):
            send_rho(now, n).wait_send()
            send_pot(now, n).wait_send()
        a, b = TOP, BOTTOM
        rest = potential(lower, 0, gain - 1.0, before(now, a + 1, b), None, a + 1, b)
        here = jnp.concatenate([lower.psi[0, a : a + 1], rest], 0)
        after = jnp.concatenate([rest, lower.psi[0, b : b + 1]], 0)
        update(lower, 0, 0, final, INNER, here, lower.psi[1, a:b], after)
        here, after = upper.psi[0, a:b], upper.psi[0, a + 1 : b + 1]
        update(upper, 0, T - 1, final, INNER, here, plane_above(now, gain, a, b), after, end_scale, end_pull)
        if not final:
            emit_inner(later, 2.0)

    def middle_pair(u, now, later, gain, final, meet):
        keep = gain - 1.0
        if meet:
            send_pot_last(now).wait_recv()
        else:
            send_fx_rows(now, u + 1).wait_recv()
            send_pot_rows(now, u + 1).wait_recv()
        send_fx_rows(now, u).wait_send()
        send_pot_rows(now, u).wait_send()
        lower_row = halo_row(lower, u, now, 2 * u, gain)
        upper_row = halo_row(upper, u, now, 2 * u + 3, gain)
        upper_below = lower.rho[u] if meet else upper.rho[u + 1]
        upper_here = potential(upper, u, keep, upper_below, fx_rows[now, 2 * u + 1])
        lower_above = upper_here if meet else potential(lower, u + 1, keep, lower.rho[u], fx_rows[now, 2 * u + 2])
        lower_here, upper_above = lower.psi[u], upper.psi[u - 1]
        whole = ((0, R),)
        after = jnp.concatenate([lower_here[1:R], lower_row[None]], 0)
        update(lower, u, u, final, whole, lower_here, lower_above, after)
        after = jnp.concatenate([upper_here[1:R], upper_row[None]], 0)
        update(upper, u, T - 1 - u, final, whole, upper_here, upper_above, after)
        if not final:
            emit(later, u, 2.0)

    def iteration(now, later, gain, final):
        outer_rows(now, later, gain, final)

        def pair(u, carry):
            @pl.when(u == 2)
            def _():
                inner_rows(now, later, gain, final)

            middle_pair(u, now, later, gain, final, False)
            return carry

        lax.fori_loop(1, PAIRS - 1, pair, 0)
        middle_pair(PAIRS - 1, now, later, gain, final, True)
        send_pot_last(now).wait_send()
        if not final:
            emit_last(later, 2.0)

    def step(k, carry):
        gain = jnp.where(k == 1, 1.0, 2.0).astype(jnp.float32)
        iteration(lax.rem(k - 1, 2), lax.rem(k, 2), gain, False)
        return carry

    lax.fori_loop(1, ITERS, step, 0)
    iteration((ITERS - 1) % 2, None, 2.0, True)


def write_kernel(*refs):
    results, targets, sem = refs[:5], refs[5:10], refs[10]
    for n in range(5):
        pltpu.make_async_copy(results[n], targets[n], sem.at[n]).start()
    for n in range(5):
        pltpu.make_async_copy(results[n], targets[n], sem.at[n]).wait()


def to_rows(x):
    planes = x.shape[0]
    return x.reshape(planes, R // 8, 8, 8, 128).transpose(0, 1, 3, 2, 4).reshape(planes * R * 8, 128)


def in_hbm(x):
    return pltpu.with_memory_space_constraint(x, pltpu.HBM)


def from_rows(x):
    return x.reshape(T, R // 8, 8, 8, 128).transpose(0, 1, 3, 2, 4).reshape(T, R, 1024)


def solution(mesh):
    sizes = mesh.shape["tm"], mesh.shape["space"]
    f32 = jnp.float32
    vmem = pltpu.VMEM
    dma = pltpu.SemaphoreType.DMA

    def body(density, flux_x, flux_y, source, potential, start_density, end_density):
        anywhere = pl.BlockSpec(memory_space=pltpu.HBM)
        on_chip = pl.BlockSpec(memory_space=vmem)
        rows = T * R * 8
        results = pl.pallas_call(
            functools.partial(kernel, sizes),
            out_shape=[vmem((rows, 128), f32)] * 5,
            in_specs=[anywhere] * 7,
            out_specs=[on_chip] * 5,
            scratch_shapes=[
                vmem((5, rows, 128), f32),
                vmem((2, R * 8, 128), f32),
                [vmem((PAIRS, R) + TILE, f32)] * 7,
                [vmem((PAIRS, R) + TILE, f32)] * 7,
                vmem((R,) + TILE, f32),
                vmem((R,) + TILE, f32),
                vmem((R,) + TILE, f32),
                vmem((2 * PAIRS,) + TILE, f32),
                vmem((2 * PAIRS + 2,) + TILE, f32),
                vmem((2, R) + TILE, f32),
                vmem((2, R) + TILE, f32),
                vmem((2, 2 * PAIRS) + TILE, f32),
                vmem((2, 2 * PAIRS + 2) + TILE, f32),
                vmem((2,) + TILE, f32),
                vmem((2,) + TILE, f32),
                dma((5, T)),
                dma((2,)),
                dma((10,)),
                dma((PAIRS,)),
                dma((PAIRS + 1,)),
                dma((2, 10)),
                dma((2, PAIRS)),
                dma((2, PAIRS + 1)),
            ],
            compiler_params=pltpu.CompilerParams(
                collective_id=0, has_side_effects=True, vmem_limit_bytes=24 << 20
            ),
        )(
            *(in_hbm(to_rows(x)) for x in (density, flux_x, flux_y, source, potential)),
            in_hbm(to_rows(start_density[None])),
            in_hbm(to_rows(end_density[None])),
        )
        results = pl.pallas_call(
            write_kernel,
            out_shape=[jax.ShapeDtypeStruct((rows, 128), f32)] * 5,
            in_specs=[on_chip] * 5,
            out_specs=[anywhere] * 5,
            scratch_shapes=[dma((5,))],
            compiler_params=pltpu.CompilerParams(vmem_limit_bytes=1 << 20),
        )(*results)
        return tuple(from_rows(x) for x in results)

    volume, plane = P("tm", "space", None), P("space", None)
    return jax.shard_map(
        body, mesh=mesh, in_specs=(volume,) * 5 + (plane,) * 2, out_specs=(volume,) * 5, check_vma=False
    )
```

```python
import collections
import functools

import jax
import jax.numpy as jnp
from jax import lax
from jax.experimental import pallas as pl
from jax.experimental.pallas import tpu as pltpu
from jax.sharding import PartitionSpec as P

NEWTON = 8
ITERS = 6

tau_step = 0.04
end_weight = 10.0

T = 16
R = 16
PAIRS = T // 2
TOP, BOTTOM = 4, 12
OUTER, INNER = ((0, TOP), (BOTTOM, R)), ((TOP, BOTTOM),)
RHO_PARTS = (0, TOP), (BOTTOM, R), (TOP, TOP + 1), (TOP + 1, BOTTOM)
POT_PARTS = (0, TOP), (BOTTOM + 1, R), (BOTTOM, BOTTOM + 1), (TOP, BOTTOM)
TILE = (8, 128)
MESH = pl.DeviceIdType.MESH


Half = collections.namedtuple("Half", ("rho", "fx", "fy", "src", "part", "pot", "psi"))


def take(ref, u, parts):
    values = [ref[u, a:b] for a, b in parts]
    return values[0] if len(values) == 1 else jnp.concatenate(values, 0)


def put(ref, u, parts, value):
    done = 0
    for a, b in parts:
        ref[u, a:b] = value[done : done + b - a]
        done += b - a


def previous_column(x):
    moved = pltpu.roll(x, 1, 2)
    lane = lax.broadcasted_iota(jnp.int32, x.shape, 2)
    return jnp.where(lane == 0, pltpu.roll(moved, 1, 1), moved)


def next_column(x):
    moved = pltpu.roll(x, 127, 2)
    lane = lax.broadcasted_iota(jnp.int32, x.shape, 2)
    return jnp.where(lane == 127, pltpu.roll(moved, 7, 1), moved)


unit = 1.0 / tau_step


def newton(top, energy):
    half = 0.5 * energy
    thrice = energy + half
    q = jnp.maximum(top, 1.0)
    top = jnp.maximum(top, 1.0 - half)
    for repeat in range(NEWTON):
        square = q * q
        q = (top * square + thrice) / (square * q + energy) * q
    q = jnp.maximum(q, 1.0)
    return q, (q - 1.0) / q


def kernel(
    sizes,
    rho_in, fx_in, fy_in, src_in, pot_in, start_in, end_in,
    rho_out, fx_out, fy_out, src_out, pot_out,
    raw, edge, lower_refs, upper_refs, start, end,
    plane_out, fx_rows_out, pot_rows_out,
    rho_halo, pot_halo, fx_rows, pot_rows, fx_corner, rho_corner,
    in_sem, edge_sem,
    plane_send, fx_send, pot_send,
    plane_recv, fx_recv, pot_recv,
):
    lower, upper = Half(*lower_refs), Half(*upper_refs)
    n_time, n_space = sizes
    me_time, me_space = lax.axis_index("tm"), lax.axis_index("space")
    time_next = lax.rem(me_time + 1, n_time)
    time_prev = lax.rem(me_time + n_time - 1, n_time)
    space_next = lax.rem(me_space + 1, n_space)
    space_prev = lax.rem(me_space + n_space - 1, n_space)
    first = me_time == 0
    last = me_time == n_time - 1

    fields_in = (rho_in, fx_in, fy_in, src_in, pot_in)
    fields_out = (rho_out, fx_out, fy_out, src_out, pot_out)
    plane_rows = R * 8

    def plane_in(n, t):
        rows = pl.ds(t * plane_rows, plane_rows)
        return pltpu.make_async_copy(fields_in[n].at[rows], raw.at[n, rows], in_sem.at[n, t])

    def edge_in(n):
        return pltpu.make_async_copy((start_in, end_in)[n], edge.at[n], edge_sem.at[n])

    barrier = pltpu.get_barrier_semaphore()
    partners = (
        (time_next, me_space), (time_prev, me_space),
        (me_time, space_next), (me_time, space_prev),
        (time_prev, space_next), (time_next, space_prev),
    )
    for partner in partners:
        pl.semaphore_signal(barrier, inc=1, device_id=partner, device_id_type=MESH)

    for u in range(PAIRS):
        for t in (u, T - 1 - u):
            for n in range(5):
                plane_in(n, t).start()
        if u == 0:
            for n in range(2):
                edge_in(n).start()

    def send(source, target, send_sem, recv_sem, device):
        return pltpu.make_async_remote_copy(
            src_ref=source, dst_ref=target, send_sem=send_sem, recv_sem=recv_sem,
            device_id=device, device_id_type=MESH,
        )

    def send_rho(slot, n):
        a, b = RHO_PARTS[n]
        rows = pl.ds(a, b - a)
        return send(
            upper.rho.at[0, rows], rho_halo.at[slot, rows], plane_send.at[n], plane_recv.at[slot, n], (time_next, me_space)
        )

    def send_pot(slot, n):
        a, b = POT_PARTS[n]
        rows = pl.ds(a, b - a)
        return send(
            plane_out.at[rows], pot_halo.at[slot, rows], plane_send.at[4 + n], plane_recv.at[slot, 4 + n], (time_prev, me_space)
        )

    def send_fx_corner(slot):
        return send(fx_rows_out.at[0], fx_corner.at[slot], plane_send.at[8], plane_recv.at[slot, 8], (time_prev, space_next))

    def send_rho_corner(slot):
        return send(upper.rho.at[0, 0], rho_corner.at[slot], plane_send.at[9], plane_recv.at[slot, 9], (time_next, space_prev))

    def send_fx_rows(slot, u):
        rows = pl.ds(2 * u, 2)
        return send(fx_rows_out.at[rows], fx_rows.at[slot, rows], fx_send.at[u], fx_recv.at[slot, u], (me_time, space_next))

    def send_pot_rows(slot, u):
        rows = pl.ds(2 * u, 2)
        return send(pot_rows_out.at[rows], pot_rows.at[slot, rows], pot_send.at[u], pot_recv.at[slot, u], (me_time, space_prev))

    def send_pot_first(slot):
        rows = pl.ds(0, 1)
        return send(pot_rows_out.at[rows], pot_rows.at[slot, rows], pot_send.at[0], pot_recv.at[slot, 0], (me_time, space_prev))

    def send_pot_last(slot):
        rows = pl.ds(2 * PAIRS + 1, 1)
        return send(
            pot_rows_out.at[rows], pot_rows.at[slot, rows], pot_send.at[PAIRS], pot_recv.at[slot, PAIRS], (me_time, space_prev)
        )

    def emit_outer(slot, gain):
        part, pot, fx = lower.part, lower.pot, lower.fx
        fx_rows_out[0] = fx[0, R - 1]
        fx_rows_out[1] = upper.fx[0, R - 1]
        held = jnp.where(first, start[0], jnp.zeros(TILE, jnp.float32))
        pot_rows_out[0] = pot[0, 0] + gain * (part[0, 0] - held)
        plane_out[0] = pot[0, 0] + gain * part[0, 0]
        for a, b in ((1, TOP), (BOTTOM + 1, R)):
            plane_out[a:b] = pot[0, a:b] + gain * (part[0, a:b] - fx[0, a - 1 : b - 1])
        send_fx_corner(slot).start()
        send_rho_corner(slot).start()
        send_fx_rows(slot, 0).start()
        send_pot_first(slot).start()
        for n in (0, 1):
            send_pot(slot, n).start()
            send_rho(slot, n).start()

    def emit_inner(slot, gain):
        part, pot, fx = lower.part, lower.pot, lower.fx
        a, b = TOP, BOTTOM + 1
        plane_out[a:b] = pot[0, a:b] + gain * (part[0, a:b] - fx[0, a - 1 : b - 1])
        for n in (2, 3):
            send_pot(slot, n).start()
            send_rho(slot, n).start()

    def emit(slot, u, gain):
        fx_rows_out[2 * u] = lower.fx[u, R - 1]
        fx_rows_out[2 * u + 1] = upper.fx[u, R - 1]
        pot_rows_out[2 * u] = lower.pot[u, 0] + gain * (lower.part[u, 0] - lower.rho[u - 1, 0])
        pot_rows_out[2 * u + 1] = upper.pot[u - 1, 0] + gain * (upper.part[u - 1, 0] - upper.rho[u, 0])
        send_fx_rows(slot, u).start()
        send_pot_rows(slot, u).start()

    def emit_last(slot, gain):
        u = PAIRS - 1
        pot_rows_out[2 * PAIRS + 1] = upper.pot[u, 0] + gain * (upper.part[u, 0] - lower.rho[u, 0])
        send_pot_last(slot).start()

    for n, ref in enumerate((start, end)):
        edge_in(n).wait()
        for i in range(R):
            value = edge[n, pl.ds((i // 8) * 64 + i % 8, 8, stride=8), :]
            ref[i] = value * unit + (1.0 if n == 0 else 0.0)

    def load_plane(t, half, u):
        for n in range(5):
            plane_in(n, t).wait()
        for i in range(R):
            rows = pl.ds(t * plane_rows + (i // 8) * 64 + i % 8, 8, stride=8)
            d, x, y, s, p = (unit * raw[n, rows, :] for n in range(5))
            d = d + 1.0
            half.rho[u, i] = d
            half.fx[u, i] = x
            half.fy[u, i] = y
            half.src[u, i] = s
            half.pot[u, i] = p
            half.part[u, i] = d + x + (y - previous_column(y[None])[0]) - s

    load_plane(0, lower, 0)
    load_plane(T - 1, upper, 0)
    pl.semaphore_wait(barrier, len(partners))
    emit_outer(0, 1.0)
    emit_inner(0, 1.0)

    def load_pair(u, carry):
        load_plane(u, lower, u)
        load_plane(T - 1 - u, upper, u)
        emit(0, u, 1.0)
        return carry

    lax.fori_loop(1, PAIRS, load_pair, 0)
    emit_last(0, 1.0)

    def potential(half, u, keep, below, row, a=0, b=R):
        if a == 0:
            beside = jnp.concatenate([row[None], half.fx[u, 0 : b - 1]], 0)
        else:
            beside = half.fx[u, a - 1 : b - 1]
        gap = half.part[u, a:b] - (below + beside)
        base = half.pot[u, a:b] + keep * gap
        half.pot[u, a:b] = base
        new = tau_step * (base + gap)
        half.psi[u, a:b] = new
        return new

    def update(half, u, t, final, parts, here, above, after, end_scale=None, end_pull=None):
        top = take(half.rho, u, parts) - (here - above)
        moved_fx = take(half.fx, u, parts) - (here - after)
        moved_fy = take(half.fy, u, parts) - (here - next_column(here))
        moved_src = take(half.src, u, parts) + here
        energy = moved_fx * moved_fx + moved_fy * moved_fy + moved_src * moved_src
        if end_scale is not None:
            ends = jnp.concatenate([end[a:b] for a, b in parts], 0)
            top = (top - 1.0 + end_pull * ends) * end_scale + 1.0
            energy = energy * end_scale
        q, factor = newton(top, energy)
        new_fx, new_fy, new_src = factor * moved_fx, factor * moved_fy, factor * moved_src
        if final:
            results = tau_step * (q - 1.0), tau_step * new_fx, tau_step * new_fy, tau_step * new_src, here
            numbers = [i for a, b in parts for i in range(a, b)]
            for ref, value in zip((rho_out, fx_out, fy_out, src_out, pot_out), results):
                for n, i in enumerate(numbers):
                    ref[pl.ds(t * plane_rows + (i // 8) * 64 + i % 8, 8, stride=8), :] = value[n]
        else:
            new_part = q + new_fx + (new_fy - previous_column(new_fy)) - new_src
            for ref, value in zip(half[:5], (q, new_fx, new_fy, new_src, new_part)):
                put(ref, u, parts, value)

    def halo_row(half, u, slot, row, gain, corner=None):
        held = half.fx[u, R - 1]
        if corner is not None:
            held = held + corner
        return tau_step * (pot_rows[slot, row] - gain * held)

    def before(now, a, b):
        return jnp.where(first, start[a:b], rho_halo[now, a:b])

    def plane_above(now, gain, a, b):
        value = tau_step * (pot_halo[now, a:b] - gain * upper.rho[0, a:b])
        if a == 0:
            corner = tau_step * (gain * fx_corner[now])
            value = jnp.concatenate([value[0:1] - corner[None], value[1:]], 0)
        return jnp.where(last, jnp.zeros_like(value), value)

    end_scale = jnp.where(last, 1.0 / (1.0 + tau_step * end_weight), 1.0).astype(jnp.float32)
    end_pull = jnp.where(last, tau_step * end_weight, 0.0).astype(jnp.float32)

    def outer_rows(now, later, gain, final):
        keep = gain - 1.0
        send_fx_rows(now, 0).wait_recv()
        send_fx_rows(now, 1).wait_recv()
        send_fx_corner(now).wait_recv()
        send_pot_first(now).wait_recv()
        send_pot_rows(now, 1).wait_recv()
        send_rho_corner(now).wait_recv()
        for n in (0, 1, 2):
            send_rho(now, n).wait_recv()
            send_pot(now, n).wait_recv()
        for n in (0, 1):
            send_rho(now, n).wait_send()
            send_pot(now, n).wait_send()
        send_fx_corner(now).wait_send()
        send_rho_corner(now).wait_send()
        send_fx_rows(now, 0).wait_send()
        send_pot_first(now).wait_send()
        lower_row = halo_row(lower, 0, now, 0, gain, jnp.where(first, jnp.zeros(TILE, jnp.float32), rho_corner[now]))
        upper_row = halo_row(upper, 0, now, 3, gain)
        lower_above = potential(lower, 1, keep, lower.rho[0], fx_rows[now, 2])
        upper_here = potential(upper, 0, keep, upper.rho[1], fx_rows[now, 1])
        over = potential(lower, 0, keep, before(now, 0, TOP + 1), fx_rows[now, 0], 0, TOP + 1)
        under = potential(lower, 0, keep, before(now, BOTTOM, R), None, BOTTOM, R)
        here = jnp.concatenate([over[0:TOP], under], 0)
        after = jnp.concatenate([over[1 : TOP + 1], under[1:], lower_row[None]], 0)
        above = jnp.concatenate([lower_above[0:TOP], lower_above[BOTTOM:R]], 0)
        update(lower, 0, 0, final, OUTER, here, above, after)
        here = jnp.concatenate([upper_here[0:TOP], upper_here[BOTTOM:R]], 0)
        after = jnp.concatenate([upper_here[1 : TOP + 1], upper_here[BOTTOM + 1 : R], upper_row[None]], 0)
        above = jnp.concatenate([plane_above(now, gain, 0, TOP), plane_above(now, gain, BOTTOM, R)], 0)
        update(upper, 0, T - 1, final, OUTER, here, above, after, end_scale, end_pull)
        if not final:
            emit_outer(later, 2.0)

    def inner_waits(now):
        send_rho(now, 3).wait_recv()
        send_pot(now, 3).wait_recv()
        for n in (2, 3):
            send_rho(now, n).wait_send()
            send_pot(now, n).wait_send()

    def inner_rows(now, gain, final):
        a, b = TOP, BOTTOM
        rest = potential(lower, 0, gain - 1.0, before(now, a + 1, b), None, a + 1, b)
        here = jnp.concatenate([lower.psi[0, a : a + 1], rest], 0)
        after = jnp.concatenate([rest, lower.psi[0, b : b + 1]], 0)
        update(lower, 0, 0, final, INNER, here, lower.psi[1, a:b], after)
        here, after = upper.psi[0, a:b], upper.psi[0, a + 1 : b + 1]
        update(upper, 0, T - 1, final, INNER, here, plane_above(now, gain, a, b), after, end_scale, end_pull)

    def middle_pair(u, now, later, gain, final, meet, inner=False):
        keep = gain - 1.0
        if inner:
            inner_waits(now)
        if meet:
            send_pot_last(now).wait_recv()
        else:
            send_fx_rows(now, u + 1).wait_recv()
            send_pot_rows(now, u + 1).wait_recv()
        send_fx_rows(now, u).wait_send()
        send_pot_rows(now, u).wait_send()
        lower_row = halo_row(lower, u, now, 2 * u, gain)
        upper_row = halo_row(upper, u, now, 2 * u + 3, gain)
        upper_below = lower.rho[u] if meet else upper.rho[u + 1]
        upper_here = potential(upper, u, keep, upper_below, fx_rows[now, 2 * u + 1])
        lower_above = upper_here if meet else potential(lower, u + 1, keep, lower.rho[u], fx_rows[now, 2 * u + 2])
        lower_here, upper_above = lower.psi[u], upper.psi[u - 1]
        if inner:
            inner_rows(now, gain, final)
        whole = ((0, R),)
        after = jnp.concatenate([lower_here[1:R], lower_row[None]], 0)
        update(lower, u, u, final, whole, lower_here, lower_above, after)
        after = jnp.concatenate([upper_here[1:R], upper_row[None]], 0)
        update(upper, u, T - 1 - u, final, whole, upper_here, upper_above, after)
        if not final:
            emit(later, u, 2.0)
            if inner:
                emit_inner(later, 2.0)

    def iteration(now, later, gain, final):
        outer_rows(now, later, gain, final)

        def pair(u, carry):
            middle_pair(u, now, later, gain, final, False)
            return carry

        middle_pair(1, now, later, gain, final, False)
        middle_pair(2, now, later, gain, final, False, True)
        lax.fori_loop(3, PAIRS - 1, pair, 0)
        middle_pair(PAIRS - 1, now, later, gain, final, True)
        send_pot_last(now).wait_send()
        if not final:
            emit_last(later, 2.0)

    def step(k, carry):
        gain = jnp.where(k == 1, 1.0, 2.0).astype(jnp.float32)
        iteration(lax.rem(k - 1, 2), lax.rem(k, 2), gain, False)
        return carry

    lax.fori_loop(1, ITERS, step, 0)
    iteration((ITERS - 1) % 2, None, 2.0, True)


def write_kernel(*refs):
    results, targets, sem = refs[:5], refs[5:10], refs[10]
    for n in range(5):
        pltpu.make_async_copy(results[n], targets[n], sem.at[n]).start()
    for n in range(5):
        pltpu.make_async_copy(results[n], targets[n], sem.at[n]).wait()


def to_rows(x):
    planes = x.shape[0]
    return x.reshape(planes, R // 8, 8, 8, 128).transpose(0, 1, 3, 2, 4).reshape(planes * R * 8, 128)


def in_hbm(x):
    return pltpu.with_memory_space_constraint(x, pltpu.HBM)


def from_rows(x):
    return x.reshape(T, R // 8, 8, 8, 128).transpose(0, 1, 3, 2, 4).reshape(T, R, 1024)


def solution(mesh):
    sizes = mesh.shape["tm"], mesh.shape["space"]
    f32 = jnp.float32
    vmem = pltpu.VMEM
    dma = pltpu.SemaphoreType.DMA

    def body(density, flux_x, flux_y, source, potential, start_density, end_density):
        anywhere = pl.BlockSpec(memory_space=pltpu.HBM)
        on_chip = pl.BlockSpec(memory_space=vmem)
        rows = T * R * 8
        results = pl.pallas_call(
            functools.partial(kernel, sizes),
            out_shape=[vmem((rows, 128), f32)] * 5,
            in_specs=[anywhere] * 7,
            out_specs=[on_chip] * 5,
            scratch_shapes=[
                vmem((5, rows, 128), f32),
                vmem((2, R * 8, 128), f32),
                [vmem((PAIRS, R) + TILE, f32)] * 7,
                [vmem((PAIRS, R) + TILE, f32)] * 7,
                vmem((R,) + TILE, f32),
                vmem((R,) + TILE, f32),
                vmem((R,) + TILE, f32),
                vmem((2 * PAIRS,) + TILE, f32),
                vmem((2 * PAIRS + 2,) + TILE, f32),
                vmem((2, R) + TILE, f32),
                vmem((2, R) + TILE, f32),
                vmem((2, 2 * PAIRS) + TILE, f32),
                vmem((2, 2 * PAIRS + 2) + TILE, f32),
                vmem((2,) + TILE, f32),
                vmem((2,) + TILE, f32),
                dma((5, T)),
                dma((2,)),
                dma((10,)),
                dma((PAIRS,)),
                dma((PAIRS + 1,)),
                dma((2, 10)),
                dma((2, PAIRS)),
                dma((2, PAIRS + 1)),
            ],
            compiler_params=pltpu.CompilerParams(
                collective_id=0, has_side_effects=True, vmem_limit_bytes=24 << 20
            ),
        )(
            *(in_hbm(to_rows(x)) for x in (density, flux_x, flux_y, source, potential)),
            in_hbm(to_rows(start_density[None])),
            in_hbm(to_rows(end_density[None])),
        )
        results = pl.pallas_call(
            write_kernel,
            out_shape=[jax.ShapeDtypeStruct((rows, 128), f32)] * 5,
            in_specs=[on_chip] * 5,
            out_specs=[anywhere] * 5,
            scratch_shapes=[dma((5,))],
            compiler_params=pltpu.CompilerParams(vmem_limit_bytes=1 << 20),
        )(*results)
        return tuple(from_rows(x) for x in results)

    volume, plane = P("tm", "space", None), P("space", None)
    return jax.shard_map(
        body, mesh=mesh, in_specs=(volume,) * 5 + (plane,) * 2, out_specs=(volume,) * 5, check_vma=False
    )
```
